32 devices in a mesh: gx: 2 (over y), gy: 4 (over x, core), gz: 4 (over z).
Axes of the slice: x: 2, y: 2, z: 4, core: 2. Of those that a mesh axis runs over, the one named last changes fastest.
Arguments:
- snapshot: float32 [12, 1024, 8, 512], P(None, 'gz', 'gx', 'gy'), may hold values from -108 to 108
- species_pick: int32 [8], replicated, may hold values from 0 to 11, as said below
- basis_start: float32 [1024, 384], replicated, may hold values from -0.1875 to 0.1875
Outputs:
- gram_matrix: float32 [1024, 1024], P(('gx', 'gy', 'gz'))
- basis: float32 [1024, 384], P(('gx', 'gy', 'gz'))
- core_tensor: float32 [8, 384, 8, 512], P(None, None, ('gx', 'gz'), 'gy')
The draws below stay inside these ranges and needn't reach their ends.
Inputs may be any that keep to these rules, and one draw needn't show every extreme that they name: `species_pick`: 8 distinct species numbers; 0 and 11 are always among them.
All inputs are finite; a program needn't handle non-finite values.
Results may differ from the reference program's by a relative error of at most 0.0003.
Values sent between devices are 32-bit elements; how exact they have to be, the bound alone decides.
A program may use at most 128 MiB of HBM per device.

```python
import math
import jax
import jax.numpy as jnp
from jax import lax

NX = 1024
RANK = 384
NSTORE = 12
S = 8
NY = 8
NZ = 512


def draw_snapshot(key, part):
    keys = jax.random.split(key, 4)
    shape = (NSTORE, NX, NY, NZ)
    noise = jnp.clip(jax.random.normal(keys[0], shape, jnp.float32), -6.0, 6.0)
    row_scale = jnp.exp(jax.random.uniform(keys[1], (NX,), jnp.float32, math.log(0.3), math.log(3.0)))
    species_scale = jnp.exp(jax.random.uniform(keys[2], (NSTORE,), jnp.float32, math.log(0.5), math.log(2.0)))
    cell_scale = jnp.exp(jax.random.uniform(keys[3], (NY, NZ), jnp.float32, math.log(0.3), math.log(3.0)))
    return noise * species_scale[:, None, None, None] * row_scale[None, :, None, None] * cell_scale[None, None, :, :]


def draw_species_pick(key, part):
    inner_pick = jax.random.permutation(jax.random.fold_in(key, 11), NSTORE - 2)[:S - 2] + 1
    ends = jnp.array([0, NSTORE - 1], jnp.int32)
    chosen = jnp.concatenate([ends, inner_pick.astype(jnp.int32)])
    return jax.random.permutation(jax.random.fold_in(key, 12), chosen).astype(jnp.int32)


def bell_draw(rng, extent, scale, limit, dtype=jnp.bfloat16):
    return jnp.clip(scale * jax.random.normal(rng, extent, jnp.float32), -limit, limit).astype(dtype)


def setup_inputs(seed: int = 0) -> dict:
    key_of = jax.random.split(jax.random.key(seed), 4)
    return {
        "snapshot": draw_snapshot(jax.random.fold_in(key_of[3], 71), 0),
        "species_pick": draw_species_pick(jax.random.fold_in(key_of[3], 71), 0),
        "basis_start": bell_draw(key_of[2], (NX, RANK), NX ** -0.5, 0.1875, jnp.float32),
    }


def reference(snapshot, species_pick, basis_start):
    highest = lax.Precision.HIGHEST

    def accumulate(position, total):
        chosen = lax.dynamic_index_in_dim(snapshot, species_pick[position], 0, keepdims=False)
        columns = chosen.reshape(NX, NY * NZ)
        return total + jnp.dot(columns.astype(jnp.float32), columns.T.astype(jnp.float32), precision=highest, preferred_element_type=jnp.float32)
    gram_total = lax.fori_loop(0, S, accumulate, jnp.zeros((NX, NX), jnp.float32))
    gram_matrix = gram_total / (S * NY * NZ)
    image_full = jnp.dot(gram_matrix, basis_start, precision=highest)
    inner_gram = jnp.dot(image_full.T, image_full, precision=highest)
    lower_factor = jnp.linalg.cholesky(inner_gram)
    basis = jax.scipy.linalg.solve_triangular(lower_factor, image_full.T, lower=True).T

    def project(species_index):
        chosen = lax.dynamic_index_in_dim(snapshot, species_index, 0, keepdims=False)
        return jnp.einsum('xr,xyz->ryz', basis, chosen, precision=highest)
    core_tensor = lax.map(project, species_pick)
    return (gram_matrix, basis, core_tensor)
```

```python
import jax
import jax.numpy as jnp
from jax import lax
from jax.experimental import pallas as pl
from jax.experimental.pallas import tpu as pltpu
from jax.sharding import PartitionSpec as P

HIGHEST = lax.Precision.HIGHEST
F32 = jnp.float32
BF16 = jnp.bfloat16
BLOCK = 128
TILE = 8


def split(x):
    high = x.astype(BF16)
    return high, (x - high.astype(F32)).astype(BF16)


def dot(a, b, contract, precision=None):
    return lax.dot_general(
        a, b, (((contract[0],), (contract[1],)), ((), ())),
        precision=precision, preferred_element_type=F32,
    )


def eliminate(read):
    count = BLOCK // TILE
    row = lax.broadcasted_iota(jnp.int32, (TILE, BLOCK), 0)
    lane = lax.broadcasted_iota(jnp.int32, (TILE, BLOCK), 1)
    left = [read(i) for i in range(count)]
    right = [(lane == row + TILE * i).astype(F32) for i in range(count)]

    def wide(x):
        return jnp.broadcast_to(x, (TILE, BLOCK))

    for t in range(count):
        columns = [wide(left[t][:, TILE * t + l:TILE * t + l + 1]) for l in range(TILE)]
        pivots, inverses, upper, lrows, rrows = [], [], [], [], []
        for l in range(TILE):
            pivot = wide(columns[l][l:l + 1, :])
            inverse = 1.0 / pivot
            factor = jnp.where(row > l, columns[l] * inverse, 0.0)
            lrow, rrow = wide(left[t][l:l + 1, :]), wide(right[t][l:l + 1, :])
            ahead = {}
            for m in range(l + 1, TILE):
                ahead[m] = wide(columns[m][l:l + 1, :])
                columns[m] = columns[m] - factor * ahead[m]
            left[t] = left[t] - factor * lrow
            right[t] = right[t] - factor * rrow
            pivots.append(pivot)
            inverses.append(inverse)
            upper.append(ahead)
            lrows.append(lrow)
            rrows.append(rrow)
        for i in range(t + 1, count):
            below = [wide(left[i][:, TILE * t + l:TILE * t + l + 1]) for l in range(TILE)]
            for l in range(TILE):
                factor = below[l] * inverses[l]
                for m in range(l + 1, TILE):
                    below[m] = below[m] - factor * upper[l][m]
                left[i] = left[i] - factor * lrows[l]
                right[i] = right[i] - factor * rrows[l]
        diagonal = pivots[0]
        for l in range(1, TILE):
            diagonal = jnp.where(row == l, pivots[l], diagonal)
        scale = lax.rsqrt(diagonal)
        scale = scale * (1.5 - 0.5 * diagonal * scale * scale)
        right[t] = right[t] * scale
    return right


def tail_kernel(image_ref, rows_ref, panel_ref, basis_ref, core_ref, a_ref, n_ref, w_ref):
    rank = image_ref.shape[1]
    blocks = rank // BLOCK
    image = image_ref[...]
    inner = dot(image, image, (0, 0), HIGHEST)
    for r in range(blocks):
        for c in range(blocks):
            a_ref[r, c] = inner[r * BLOCK:(r + 1) * BLOCK, c * BLOCK:(c + 1) * BLOCK]
            if r != c:
                n_ref[r, c] = jnp.zeros((BLOCK, BLOCK), F32)
            else:
                n_ref[r, c] = (
                    lax.broadcasted_iota(jnp.int32, (BLOCK, BLOCK), 0)
                    == lax.broadcasted_iota(jnp.int32, (BLOCK, BLOCK), 1)
                ).astype(F32)

    @pl.loop(0, blocks)
    def _(b):
        tiles = eliminate(lambda i: a_ref[b, b, TILE * i:TILE * (i + 1), :])
        for i, tile in enumerate(tiles):
            w_ref[TILE * i:TILE * (i + 1), :] = tile
        w = w_ref[...]
        for c in range(blocks):
            n_ref[b, c] = dot(w, n_ref[b, c], (1, 0), HIGHEST)
        for r in range(1, blocks):
            @pl.when(r > b)
            def _():
                a_ref[b, r] = dot(w, a_ref[b, r], (1, 0), HIGHEST)
        for r in range(1, blocks):
            @pl.when(r > b)
            def _():
                factor = a_ref[b, r]
                for c in range(1, blocks):
                    @pl.when(c > b)
                    def _():
                        a_ref[r, c] = a_ref[r, c] - dot(factor, a_ref[b, c], (0, 0), HIGHEST)
                for c in range(blocks - 1):
                    n_ref[r, c] = n_ref[r, c] - dot(factor, n_ref[b, c], (0, 0), HIGHEST)

    inverse = jnp.concatenate(
        [jnp.concatenate([n_ref[r, c] for c in range(blocks)], axis=1) for r in range(blocks)],
        axis=0,
    )
    basis_ref[...] = dot(rows_ref[...], inverse, (1, 1), HIGHEST)
    basis_t = dot(inverse, image, (1, 1), HIGHEST)
    bh, bl = split(basis_t)
    for s in range(panel_ref.shape[0]):
        ph, plo = split(panel_ref[s])
        core_ref[s] = dot(bh, ph, (1, 0)) + dot(bh, plo, (1, 0)) + dot(bl, ph, (1, 0))


def tail(image, rows, panel):
    total, rank = image.shape
    species, _, width = panel.shape
    vmem = pl.BlockSpec(memory_space=pltpu.VMEM)
    blocks = rank // BLOCK
    return pl.pallas_call(
        tail_kernel,
        out_shape=(
            jax.ShapeDtypeStruct(rows.shape, F32),
            jax.ShapeDtypeStruct((species, rank, width), F32),
        ),
        in_specs=[vmem] * 3,
        out_specs=(vmem, vmem),
        scratch_shapes=[
            pltpu.VMEM((blocks, blocks, BLOCK, BLOCK), F32),
            pltpu.VMEM((blocks, blocks, BLOCK, BLOCK), F32),
            pltpu.VMEM((BLOCK, BLOCK), F32),
        ],
        compiler_params=pltpu.CompilerParams(vmem_limit_bytes=48 * 2**20),
        name="tail",
    )(image, rows, panel)


def gather_kernel(pick_ref, in_ref, out_ref):
    for y in range(in_ref.shape[2]):
        out_ref[y, 0] = in_ref[0, :, y, :]


def gather(snapshot, species_pick):
    _, rows, ys, width = snapshot.shape
    species = species_pick.shape[0]
    return pl.pallas_call(
        gather_kernel,
        out_shape=jax.ShapeDtypeStruct((ys, species, rows, width), F32),
        grid_spec=pltpu.PrefetchScalarGridSpec(
            num_scalar_prefetch=1,
            grid=(species,),
            in_specs=[pl.BlockSpec((1, rows, ys, width), lambda s, pick: (pick[s], 0, 0, 0))],
            out_specs=pl.BlockSpec((ys, 1, rows, width), lambda s, pick: (0, s, 0, 0)),
        ),
        name="gather",
    )(species_pick, snapshot)


def per_device(snapshot, species_pick, basis_start):
    axes = ("gx", "gy", "gz")
    devices = lax.axis_size(axes)
    picked = gather(snapshot, species_pick)
    ys, species, rows, width = picked.shape
    panel = lax.all_to_all(picked, "gz", split_axis=0, concat_axis=2, tiled=True)
    panel = panel.reshape(species, rows * lax.axis_size("gz"), width)
    total = panel.shape[1]
    scaling = 1.0 / (species * width * devices)
    gram_rows = lax.psum_scatter(
        jnp.einsum("sxz,swz->xw", panel, panel, precision=lax.Precision.HIGH) * scaling,
        axes, scatter_dimension=0, tiled=True,
    )
    image_rows = jnp.dot(gram_rows, basis_start, precision=HIGHEST)
    image = lax.all_gather(image_rows, axes, axis=0, tiled=True)
    basis_rows, core = tail(image, image_rows, panel)
    return gram_rows, basis_rows, core[:, :, None, :]


def solution(mesh):
    return jax.shard_map(
        per_device,
        mesh=mesh,
        in_specs=(P(None, "gz", "gx", "gy"), P(), P()),
        out_specs=(
            P(("gx", "gy", "gz"), None),
            P(("gx", "gy", "gz"), None),
            P(None, None, ("gx", "gz"), "gy"),
        ),
        check_vma=False,
    )
```

```python
import functools

import jax
import jax.numpy as jnp
from jax import lax
from jax.experimental import pallas as pl
from jax.experimental.pallas import tpu as pltpu
from jax.sharding import PartitionSpec as P

HIGHEST = lax.Precision.HIGHEST
F32 = jnp.float32
BF16 = jnp.bfloat16
BLOCK = 128
TILE = 8


def split(x):
    high = x.astype(BF16)
    return high, (x - high.astype(F32)).astype(BF16)


def dot(a, b, contract, precision=None):
    return lax.dot_general(
        a, b, (((contract[0],), (contract[1],)), ((), ())),
        precision=precision, preferred_element_type=F32,
    )


def eliminate(read):
    count = BLOCK // TILE
    row = lax.broadcasted_iota(jnp.int32, (TILE, BLOCK), 0)
    lane = lax.broadcasted_iota(jnp.int32, (TILE, BLOCK), 1)
    left = [read(i) for i in range(count)]
    right = [(lane == row + TILE * i).astype(F32) for i in range(count)]

    def wide(x):
        return jnp.broadcast_to(x, (TILE, BLOCK))

    for t in range(count):
        columns = [wide(left[t][:, TILE * t + l:TILE * t + l + 1]) for l in range(TILE)]
        pivots, inverses, upper, lrows, rrows = [], [], [], [], []
        for l in range(TILE):
            pivot = wide(columns[l][l:l + 1, :])
            inverse = 1.0 / pivot
            factor = jnp.where(row > l, columns[l] * inverse, 0.0)
            lrow, rrow = wide(left[t][l:l + 1, :]), wide(right[t][l:l + 1, :])
            ahead = {}
            for m in range(l + 1, TILE):
                ahead[m] = wide(columns[m][l:l + 1, :])
                columns[m] = columns[m] - factor * ahead[m]
            left[t] = left[t] - factor * lrow
            right[t] = right[t] - factor * rrow
            pivots.append(pivot)
            inverses.append(inverse)
            upper.append(ahead)
            lrows.append(lrow)
            rrows.append(rrow)
        for i in range(t + 1, count):
            below = [wide(left[i][:, TILE * t + l:TILE * t + l + 1]) for l in range(TILE)]
            for l in range(TILE):
                factor = below[l] * inverses[l]
                for m in range(l + 1, TILE):
                    below[m] = below[m] - factor * upper[l][m]
                left[i] = left[i] - factor * lrows[l]
                right[i] = right[i] - factor * rrows[l]
        diagonal = pivots[0]
        for l in range(1, TILE):
            diagonal = jnp.where(row == l, pivots[l], diagonal)
        scale = lax.rsqrt(diagonal)
        scale = scale * (1.5 - 0.5 * diagonal * scale * scale)
        right[t] = right[t] * scale
    return right


def tail_kernel(image_ref, rows_ref, panel_ref, basis_ref, core_ref, a_ref, n_ref, w_ref):
    rank = image_ref.shape[1]
    blocks = rank // BLOCK
    image = image_ref[...]
    inner = dot(image, image, (0, 0), HIGHEST)
    for r in range(blocks):
        for c in range(blocks):
            a_ref[r, c] = inner[r * BLOCK:(r + 1) * BLOCK, c * BLOCK:(c + 1) * BLOCK]
            if r != c:
                n_ref[r, c] = jnp.zeros((BLOCK, BLOCK), F32)
            else:
                n_ref[r, c] = (
                    lax.broadcasted_iota(jnp.int32, (BLOCK, BLOCK), 0)
                    == lax.broadcasted_iota(jnp.int32, (BLOCK, BLOCK), 1)
                ).astype(F32)

    @pl.loop(0, blocks)
    def _(b):
        tiles = eliminate(lambda i: a_ref[b, b, TILE * i:TILE * (i + 1), :])
        for i, tile in enumerate(tiles):
            w_ref[TILE * i:TILE * (i + 1), :] = tile
        w = w_ref[...]
        for c in range(blocks):
            n_ref[b, c] = dot(w, n_ref[b, c], (1, 0), HIGHEST)
        for r in range(1, blocks):
            @pl.when(r > b)
            def _():
                a_ref[b, r] = dot(w, a_ref[b, r], (1, 0), HIGHEST)
        for r in range(1, blocks):
            @pl.when(r > b)
            def _():
                factor = a_ref[b, r]
                for c in range(1, blocks):
                    @pl.when(c > b)
                    def _():
                        a_ref[r, c] = a_ref[r, c] - dot(factor, a_ref[b, c], (0, 0), HIGHEST)
                for c in range(blocks - 1):
                    n_ref[r, c] = n_ref[r, c] - dot(factor, n_ref[b, c], (0, 0), HIGHEST)

    inverse = jnp.concatenate(
        [jnp.concatenate([n_ref[r, c] for c in range(blocks)], axis=1) for r in range(blocks)],
        axis=0,
    )
    basis_ref[...] = dot(rows_ref[...], inverse, (1, 1), HIGHEST)
    basis_t = dot(inverse, image, (1, 1), HIGHEST)
    bh, bl = split(basis_t)
    for s in range(panel_ref.shape[0]):
        ph, plo = split(panel_ref[s])
        core_ref[s] = dot(bh, ph, (1, 0)) + dot(bh, plo, (1, 0)) + dot(bl, ph, (1, 0))


def tail(image, rows, panel):
    total, rank = image.shape
    species, _, width = panel.shape
    vmem = pl.BlockSpec(memory_space=pltpu.VMEM)
    blocks = rank // BLOCK
    return pl.pallas_call(
        tail_kernel,
        out_shape=(
            jax.ShapeDtypeStruct(rows.shape, F32),
            jax.ShapeDtypeStruct((species, rank, width), F32),
        ),
        in_specs=[vmem] * 3,
        out_specs=(vmem, vmem),
        scratch_shapes=[
            pltpu.VMEM((blocks, blocks, BLOCK, BLOCK), F32),
            pltpu.VMEM((blocks, blocks, BLOCK, BLOCK), F32),
            pltpu.VMEM((BLOCK, BLOCK), F32),
        ],
        compiler_params=pltpu.CompilerParams(vmem_limit_bytes=48 * 2**20),
        name="tail",
    )(image, rows, panel)


def gather_kernel(pick_ref, in_ref, out_ref):
    for y in range(in_ref.shape[2]):
        out_ref[y, 0] = in_ref[0, :, y, :]


def gather(snapshot, species_pick):
    _, rows, ys, width = snapshot.shape
    species = species_pick.shape[0]
    return pl.pallas_call(
        gather_kernel,
        out_shape=jax.ShapeDtypeStruct((ys, species, rows, width), F32),
        grid_spec=pltpu.PrefetchScalarGridSpec(
            num_scalar_prefetch=1,
            grid=(species,),
            in_specs=[pl.BlockSpec((1, rows, ys, width), lambda s, pick: (pick[s], 0, 0, 0))],
            out_specs=pl.BlockSpec((ys, 1, rows, width), lambda s, pick: (0, s, 0, 0)),
        ),
        name="gather",
    )(species_pick, snapshot)


def reduce_kernel(dims, g_ref, start_ref, rows_ref, own_ref, image_ref,
                  r0, sa, sb, ra1, rb1, ta, tb, ra2, rb2, tz, r3, im, send, recv):
    nx, nh, nl, nz = dims
    gx, gy, gz = lax.axis_index("gx"), lax.axis_index("gy"), lax.axis_index("gz")
    yh, yl = gy // nl, gy % nl
    share, total = rows_ref.shape
    group = nz * share
    half = total // 2
    zhalf = nz // 2
    peers = {
        "x": [((gx + k) % nx, "gx", lambda p: p) for k in range(1, nx)],
        "h": [((yh + k) % nh, "gy", lambda p: p * nl + yl) for k in range(1, nh)],
        "l": [((yl + k) % nl, "gy", lambda p: yh * nl + p) for k in range(1, nl)],
        "z": [((gz + k) % nz, "gz", lambda p: p) for k in range(1, nz)],
    }
    used = [0]

    barrier = pltpu.get_barrier_semaphore()
    count = 0
    for key in "xhlz":
        for p, axis, place in peers[key]:
            pl.semaphore_signal(barrier, inc=1, device_id={axis: place(p)},
                                device_id_type=pl.DeviceIdType.MESH)
            count += 1
    pl.semaphore_wait(barrier, count)

    def exchange(key, source, target):
        copies = []
        for k, (p, axis, place) in enumerate(peers[key]):
            i = used[0]
            used[0] += 1
            copy = pltpu.make_async_remote_copy(
                src_ref=source(p), dst_ref=target(k), send_sem=send.at[i], recv_sem=recv.at[i],
                device_id={axis: place(p)}, device_id_type=pl.DeviceIdType.MESH,
            )
            copy.start()
            copies.append(copy)
        return copies

    def finish(copies):
        for copy in copies:
            copy.wait()

    def plus(first, buffer, count):
        for k in range(count):
            first = first + buffer(k)
        return first

    def part(p, size):
        return pl.ds(pl.multiple_of(p * size, size), size)

    finish(exchange("l", lambda p: g_ref.at[:, part(p, group), :], lambda k: r0.at[k]))
    for m in range(nx * nh):
        v = plus(g_ref[m, part(yl, group), :], lambda k: r0[k, m], nl - 1)
        sa[m // nh, m % nh] = v[:, :half]
        sb[m % nh, m // nh] = v[:, half:]
    first_a = exchange("x", lambda p: sa.at[p], lambda k: ra1.at[k])
    first_b = exchange("h", lambda p: sb.at[p], lambda k: rb1.at[k])
    finish(first_a)
    ta[...] = plus(sa[gx], lambda k: ra1[k], nx - 1)
    second_a = exchange("h", lambda p: ta.at[p], lambda k: ra2.at[k])
    finish(first_b)
    tb[...] = plus(sb[yh], lambda k: rb1[k], nh - 1)
    second_b = exchange("x", lambda p: tb.at[p], lambda k: rb2.at[k])
    finish(second_a)
    tz[:, :half] = plus(ta[yh], lambda k: ra2[k], nh - 1)
    finish(second_b)
    tz[:, half:] = plus(tb[gx], lambda k: rb2[k], nx - 1)
    finish(exchange("z", lambda p: tz.at[part(p, share), :], lambda k: r3.at[k]))
    gram = plus(tz[part(gz, share), :], lambda k: r3[k], nz - 1)
    rows_ref[...] = gram
    own = dot(gram, start_ref[...], (1, 0), HIGHEST)
    own_ref[...] = own
    im[gx, yh, yl, gz] = own

    def spread(key, *place):
        return exchange(key, lambda p: im.at[place], lambda k: im.at[place])

    low, high, every = pl.ds(0, zhalf), pl.ds(zhalf, nz - zhalf), slice(None)
    finish(spread("z", gx, yh, yl, gz))
    first_a = spread("x", gx, yh, yl, low)
    first_b = spread("h", gx, yh, yl, high)
    finish(first_a)
    second_a = spread("h", every, yh, yl, low)
    finish(first_b)
    second_b = spread("x", gx, every, yl, high)
    finish(second_a)
    finish(second_b)
    finish(spread("l", every, every, yl))
    image_ref[...] = im[...]


def reduce_and_spread(gram, start):
    nx, ny, nz = lax.axis_size("gx"), lax.axis_size("gy"), lax.axis_size("gz")
    nl = 2 if ny % 2 == 0 else 1
    nh = ny // nl
    total, rank = start.shape
    share = total // (nx * ny * nz)
    group, half = nz * share, total // 2
    copies = 2 * ((nl - 1) + 2 * (nx - 1) + 2 * (nh - 1) + (nz - 1))
    vmem = pl.BlockSpec(memory_space=pltpu.VMEM)
    shape = (nx, nh, nl, nz, share, rank)

    def held(*size):
        return pltpu.VMEM(size, F32)

    rows, own, image = pl.pallas_call(
        functools.partial(reduce_kernel, (nx, nh, nl, nz)),
        out_shape=(
            jax.ShapeDtypeStruct((share, total), F32),
            jax.ShapeDtypeStruct((share, rank), F32),
            jax.ShapeDtypeStruct(shape, F32),
        ),
        in_specs=[vmem] * 2,
        out_specs=(vmem,) * 3,
        scratch_shapes=[
            held(max(nl - 1, 1), nx * nh, group, total),
            held(nx, nh, group, half),
            held(nh, nx, group, half),
            held(max(nx - 1, 1), nh, group, half),
            held(max(nh - 1, 1), nx, group, half),
            held(nh, group, half),
            held(nx, group, half),
            held(max(nh - 1, 1), group, half),
            held(max(nx - 1, 1), group, half),
            held(group, total),
            held(max(nz - 1, 1), share, total),
            held(*shape),
            pltpu.SemaphoreType.DMA((copies,)),
            pltpu.SemaphoreType.DMA((copies,)),
        ],
        compiler_params=pltpu.CompilerParams(
            collective_id=0, has_side_effects=True, vmem_limit_bytes=48 * 2**20),
        name="reduce_and_spread",
    )(gram.reshape(nx * nh, nl * group, total), start)
    return rows, own, image.reshape(total, rank)


def per_device(snapshot, species_pick, basis_start):
    axes = ("gx", "gy", "gz")
    devices = lax.axis_size(axes)
    picked = gather(snapshot, species_pick)
    ys, species, rows, width = picked.shape
    panel = lax.all_to_all(picked, "gz", split_axis=0, concat_axis=2, tiled=True)
    panel = panel.reshape(species, rows * lax.axis_size("gz"), width)
    scaling = 1.0 / (species * width * devices)
    gram = jnp.einsum("sxz,swz->xw", panel, panel, precision=lax.Precision.HIGH) * scaling
    gram_rows, image_rows, image = reduce_and_spread(gram, basis_start)
    basis_rows, core = tail(image, image_rows, panel)
    return gram_rows, basis_rows, core[:, :, None, :]


def solution(mesh):
    return jax.shard_map(
        per_device,
        mesh=mesh,
        in_specs=(P(None, "gz", "gx", "gy"), P(), P()),
        out_specs=(
            P(("gx", "gy", "gz"), None),
            P(("gx", "gy", "gz"), None),
            P(None, None, ("gx", "gz"), "gy"),
        ),
        check_vma=False,
    )
```

```python
import functools

import jax
import jax.numpy as jnp
from jax import lax
from jax.experimental import pallas as pl
from jax.experimental.pallas import tpu as pltpu
from jax.sharding import PartitionSpec as P

HIGHEST = lax.Precision.HIGHEST
F32 = jnp.float32
BF16 = jnp.bfloat16
BLOCK = 128
TILE = 8
PAIR = 2


def split(x):
    high = x.astype(BF16)
    return high, (x - high.astype(F32)).astype(BF16)


def dot(a, b, contract, precision=None):
    return lax.dot_general(
        a, b, (((contract[0],), (contract[1],)), ((), ())),
        precision=precision, preferred_element_type=F32,
    )


def eliminate(read):
    count = BLOCK // TILE
    row = lax.broadcasted_iota(jnp.int32, (TILE, BLOCK), 0)
    lane = lax.broadcasted_iota(jnp.int32, (TILE, BLOCK), 1)
    left = [read(i) for i in range(count)]
    right = [(lane == row + TILE * i).astype(F32) for i in range(count)]

    def wide(x):
        return jnp.broadcast_to(x, (TILE, BLOCK))

    for t in range(count):
        columns = [wide(left[t][:, TILE * t + l:TILE * t + l + 1]) for l in range(TILE)]
        pivots, inverses, upper, lrows, rrows = [], [], [], [], []
        for l in range(TILE):
            pivot = wide(columns[l][l:l + 1, :])
            inverse = 1.0 / pivot
            factor = jnp.where(row > l, columns[l] * inverse, 0.0)
            lrow, rrow = wide(left[t][l:l + 1, :]), wide(right[t][l:l + 1, :])
            ahead = {}
            for m in range(l + 1, TILE):
                ahead[m] = wide(columns[m][l:l + 1, :])
                columns[m] = columns[m] - factor * ahead[m]
            left[t] = left[t] - factor * lrow
            right[t] = right[t] - factor * rrow
            pivots.append(pivot)
            inverses.append(inverse)
            upper.append(ahead)
            lrows.append(lrow)
            rrows.append(rrow)
        for i in range(t + 1, count):
            below = [wide(left[i][:, TILE * t + l:TILE * t + l + 1]) for l in range(TILE)]
            for l in range(TILE):
                factor = below[l] * inverses[l]
                for m in range(l + 1, TILE):
                    below[m] = below[m] - factor * upper[l][m]
                left[i] = left[i] - factor * lrows[l]
                right[i] = right[i] - factor * rrows[l]
        diagonal = pivots[0]
        for l in range(1, TILE):
            diagonal = jnp.where(row == l, pivots[l], diagonal)
        scale = lax.rsqrt(diagonal)
        scale = scale * (1.5 - 0.5 * diagonal * scale * scale)
        right[t] = right[t] * scale
    return right


def tail_kernel(image_ref, rows_ref, panel_ref, basis_ref, core_ref, a_ref, n_ref, w_ref):
    rank = image_ref.shape[1]
    blocks = rank // BLOCK
    image = image_ref[...]
    inner = dot(image, image, (0, 0), HIGHEST)
    for r in range(blocks):
        for c in range(blocks):
            a_ref[r, c] = inner[r * BLOCK:(r + 1) * BLOCK, c * BLOCK:(c + 1) * BLOCK]
            if r != c:
                n_ref[r, c] = jnp.zeros((BLOCK, BLOCK), F32)
            else:
                n_ref[r, c] = (
                    lax.broadcasted_iota(jnp.int32, (BLOCK, BLOCK), 0)
                    == lax.broadcasted_iota(jnp.int32, (BLOCK, BLOCK), 1)
                ).astype(F32)

    @pl.loop(0, blocks)
    def _(b):
        tiles = eliminate(lambda i: a_ref[b, b, TILE * i:TILE * (i + 1), :])
        for i, tile in enumerate(tiles):
            w_ref[TILE * i:TILE * (i + 1), :] = tile
        w = w_ref[...]
        for c in range(blocks):
            n_ref[b, c] = dot(w, n_ref[b, c], (1, 0), HIGHEST)
        for r in range(1, blocks):
            @pl.when(r > b)
            def _():
                a_ref[b, r] = dot(w, a_ref[b, r], (1, 0), HIGHEST)
        for r in range(1, blocks):
            @pl.when(r > b)
            def _():
                factor = a_ref[b, r]
                for c in range(1, blocks):
                    @pl.when(c > b)
                    def _():
                        a_ref[r, c] = a_ref[r, c] - dot(factor, a_ref[b, c], (0, 0), HIGHEST)
                for c in range(blocks - 1):
                    n_ref[r, c] = n_ref[r, c] - dot(factor, n_ref[b, c], (0, 0), HIGHEST)

    inverse = jnp.concatenate(
        [jnp.concatenate([n_ref[r, c] for c in range(blocks)], axis=1) for r in range(blocks)],
        axis=0,
    )
    basis_ref[...] = dot(rows_ref[...], inverse, (1, 1), HIGHEST)
    basis_t = dot(inverse, image, (1, 1), HIGHEST)
    bh, bl = split(basis_t)
    for s in range(panel_ref.shape[0]):
        ph, plo = split(panel_ref[s])
        core_ref[s] = dot(bh, ph, (1, 0)) + dot(bh, plo, (1, 0)) + dot(bl, ph, (1, 0))


def tail(image, rows, panel):
    total, rank = image.shape
    species, _, width = panel.shape
    vmem = pl.BlockSpec(memory_space=pltpu.VMEM)
    blocks = rank // BLOCK
    return pl.pallas_call(
        tail_kernel,
        out_shape=(
            jax.ShapeDtypeStruct(rows.shape, F32),
            jax.ShapeDtypeStruct((species, rank, width), F32),
        ),
        in_specs=[vmem] * 3,
        out_specs=(vmem, vmem),
        scratch_shapes=[
            pltpu.VMEM((blocks, blocks, BLOCK, BLOCK), F32),
            pltpu.VMEM((blocks, blocks, BLOCK, BLOCK), F32),
            pltpu.VMEM((BLOCK, BLOCK), F32),
        ],
        compiler_params=pltpu.CompilerParams(vmem_limit_bytes=24 * 2**20),
        name="tail",
    )(image, rows, panel)


def gather_kernel(pick_ref, in_ref, out_ref):
    for y in range(in_ref.shape[2]):
        out_ref[y, 0] = in_ref[0, :, y, :]


def gather(snapshot, species_pick):
    _, rows, ys, width = snapshot.shape
    species = species_pick.shape[0]
    return pl.pallas_call(
        gather_kernel,
        out_shape=jax.ShapeDtypeStruct((ys, species, rows, width), F32),
        grid_spec=pltpu.PrefetchScalarGridSpec(
            num_scalar_prefetch=1,
            grid=(species,),
            in_specs=[pl.BlockSpec((1, rows, ys, width), lambda s, pick: (pick[s], 0, 0, 0))],
            out_specs=pl.BlockSpec((ys, 1, rows, width), lambda s, pick: (0, s, 0, 0)),
        ),
        name="gather",
    )(species_pick, snapshot)


def reduce_kernel(dims, g_ref, start_ref, rows_ref, own_ref, image_ref,
                  r0, sa, sb, ra1, rb1, ta, tb, ra2, rb2, tz, r3, im, send, recv):
    nx, nh, nl, nz = dims
    gx, gy, gz = lax.axis_index("gx"), lax.axis_index("gy"), lax.axis_index("gz")
    yh, yl = gy // nl, gy % nl
    share, total = rows_ref.shape
    group = nz * share
    half = total // 2
    zhalf = nz // 2
    peers = {
        "x": [((gx + k) % nx, "gx", lambda p: p) for k in range(1, nx)],
        "h": [((yh + k) % nh, "gy", lambda p: p * nl + yl) for k in range(1, nh)],
        "l": [((yl + k) % nl, "gy", lambda p: yh * nl + p) for k in range(1, nl)],
        "z": [((gz + k) % nz, "gz", lambda p: p) for k in range(1, nz)],
    }
    used = [0]

    barrier = pltpu.get_barrier_semaphore()
    count = 0
    for key in "xhlz":
        for p, axis, place in peers[key]:
            pl.semaphore_signal(barrier, inc=1, device_id={axis: place(p)},
                                device_id_type=pl.DeviceIdType.MESH)
            count += 1
    pl.semaphore_wait(barrier, count)

    def exchange(key, source, target):
        copies = []
        for k, (p, axis, place) in enumerate(peers[key]):
            i = used[0]
            used[0] += 1
            copy = pltpu.make_async_remote_copy(
                src_ref=source(p), dst_ref=target(k), send_sem=send.at[i], recv_sem=recv.at[i],
                device_id={axis: place(p)}, device_id_type=pl.DeviceIdType.MESH,
            )
            copy.start()
            copies.append(copy)
        return copies

    def finish(copies):
        for copy in copies:
            copy.wait()

    def plus(first, buffer, count):
        for k in range(count):
            first = first + buffer(k)
        return first

    def part(p, size):
        return pl.ds(pl.multiple_of(p * size, size), size)

    finish(exchange("l", lambda p: g_ref.at[:, part(p, group), :], lambda k: r0.at[k]))
    for m in range(nx * nh):
        v = plus(g_ref[m, part(yl, group), :], lambda k: r0[k, m], nl - 1)
        sa[m // nh, m % nh] = v[:, :half]
        sb[m % nh, m // nh] = v[:, half:]
    first_a = exchange("x", lambda p: sa.at[p], lambda k: ra1.at[k])
    first_b = exchange("h", lambda p: sb.at[p], lambda k: rb1.at[k])
    finish(first_a)
    ta[...] = plus(sa[gx], lambda k: ra1[k], nx - 1)
    second_a = exchange("h", lambda p: ta.at[p], lambda k: ra2.at[k])
    finish(first_b)
    tb[...] = plus(sb[yh], lambda k: rb1[k], nh - 1)
    second_b = exchange("x", lambda p: tb.at[p], lambda k: rb2.at[k])
    finish(second_a)
    tz[:, :half] = plus(ta[yh], lambda k: ra2[k], nh - 1)
    finish(second_b)
    tz[:, half:] = plus(tb[gx], lambda k: rb2[k], nx - 1)
    finish(exchange("z", lambda p: tz.at[part(p, share), :], lambda k: r3.at[k]))
    gram = plus(tz[part(gz, share), :], lambda k: r3[k], nz - 1)
    rows_ref[...] = gram
    own = dot(gram, start_ref[...], (1, 0), HIGHEST)
    own_ref[...] = own
    im[gx, yh, yl, gz] = own

    def spread(key, *place):
        return exchange(key, lambda p: im.at[place], lambda k: im.at[place])

    low, high, every = pl.ds(0, zhalf), pl.ds(zhalf, nz - zhalf), slice(None)
    finish(spread("z", gx, yh, yl, gz))
    first_a = spread("x", gx, yh, yl, low)
    first_b = spread("h", gx, yh, yl, high)
    finish(first_a)
    second_a = spread("h", every, yh, yl, low)
    finish(first_b)
    second_b = spread("x", gx, every, yl, high)
    finish(second_a)
    finish(second_b)
    finish(spread("l", every, every, yl))
    image_ref[...] = im[...]


def reduce_and_spread(gram, start):
    nx, ny, nz = lax.axis_size("gx"), lax.axis_size("gy"), lax.axis_size("gz")
    nl = 2 if ny % 2 == 0 else 1
    nh = ny // nl
    total, rank = start.shape
    share = total // (nx * ny * nz)
    group, half = nz * share, total // 2
    copies = 2 * ((nl - 1) + 2 * (nx - 1) + 2 * (nh - 1) + (nz - 1))
    vmem = pl.BlockSpec(memory_space=pltpu.VMEM)
    shape = (nx, nh, nl, nz, share, rank)

    def held(*size):
        return pltpu.VMEM(size, F32)

    rows, own, image = pl.pallas_call(
        functools.partial(reduce_kernel, (nx, nh, nl, nz)),
        out_shape=(
            jax.ShapeDtypeStruct((share, total), F32),
            jax.ShapeDtypeStruct((share, rank), F32),
            jax.ShapeDtypeStruct(shape, F32),
        ),
        in_specs=[vmem] * 2,
        out_specs=(vmem,) * 3,
        scratch_shapes=[
            held(max(nl - 1, 1), nx * nh, group, total),
            held(nx, nh, group, half),
            held(nh, nx, group, half),
            held(max(nx - 1, 1), nh, group, half),
            held(max(nh - 1, 1), nx, group, half),
            held(nh, group, half),
            held(nx, group, half),
            held(max(nh - 1, 1), group, half),
            held(max(nx - 1, 1), group, half),
            held(group, total),
            held(max(nz - 1, 1), share, total),
            held(*shape),
            pltpu.SemaphoreType.DMA((copies,)),
            pltpu.SemaphoreType.DMA((copies,)),
        ],
        compiler_params=pltpu.CompilerParams(
            collective_id=0, has_side_effects=True, vmem_limit_bytes=24 * 2**20),
        name="reduce_and_spread",
    )(gram.reshape(nx * nh, nl * group, total), start)
    return rows, own, image.reshape(total, rank)


def exchange_kernel(scaling, picked_ref, panel_ref, gram_ref, high, low, own_sem, send, recv):
    nz, species, rows, width = picked_ref.shape
    chunks = species // PAIR
    gz = lax.axis_index("gz")

    barrier = pltpu.get_barrier_semaphore()
    for k in range(1, nz):
        pl.semaphore_signal(barrier, inc=1, device_id={"gz": (gz + k) % nz},
                            device_id_type=pl.DeviceIdType.MESH)
    own = pltpu.make_async_copy(picked_ref.at[gz], panel_ref.at[:, gz], own_sem)
    own.start()
    pl.semaphore_wait(barrier, nz - 1)

    copies = []
    for j in range(chunks):
        for k in range(1, nz):
            p, i = (gz + k) % nz, len(copies)
            copy = pltpu.make_async_remote_copy(
                src_ref=picked_ref.at[p, pl.ds(PAIR * j, PAIR)],
                dst_ref=panel_ref.at[pl.ds(PAIR * j, PAIR), gz],
                send_sem=send.at[i], recv_sem=recv.at[i],
                device_id={"gz": p}, device_id_type=pl.DeviceIdType.MESH,
            )
            copy.start()
            copies.append(copy)
    own.wait()
    for j in range(chunks):
        for copy in copies[j * (nz - 1):(j + 1) * (nz - 1)]:
            copy.wait_recv()
        for t in range(PAIR):
            upper, lower = split(panel_ref[PAIR * j + t].reshape(nz * rows, width))
            high[:, t * width:(t + 1) * width] = upper
            low[:, t * width:(t + 1) * width] = lower

        @pl.loop(0, nz)
        def _(a):
            here = pl.ds(pl.multiple_of(a * rows, rows), rows)
            ah, al = high[here, :], low[here, :]
            for b in range(nz):
                there = slice(b * rows, (b + 1) * rows)
                bh, bl = high[there, :], low[there, :]
                part = dot(ah, bh, (1, 1)) + (dot(ah, bl, (1, 1)) + dot(al, bh, (1, 1)))
                if j > 0:
                    part = part + gram_ref[here, there]
                if j == chunks - 1:
                    part = part * scaling
                gram_ref[here, there] = part
    for copy in copies:
        copy.wait_send()


def exchange(picked, scaling):
    nz, species, rows, width = picked.shape
    total = nz * rows
    copies = species // PAIR * (nz - 1)
    vmem = pl.BlockSpec(memory_space=pltpu.VMEM)
    panel, gram = pl.pallas_call(
        functools.partial(exchange_kernel, scaling),
        out_shape=(
            jax.ShapeDtypeStruct((species, nz, rows, width), F32),
            jax.ShapeDtypeStruct((total, total), F32),
        ),
        in_specs=[pl.BlockSpec(memory_space=pltpu.HBM)],
        out_specs=(vmem, vmem),
        scratch_shapes=[
            pltpu.VMEM((total, PAIR * width), BF16),
            pltpu.VMEM((total, PAIR * width), BF16),
            pltpu.SemaphoreType.DMA,
            pltpu.SemaphoreType.DMA((copies,)),
            pltpu.SemaphoreType.DMA((copies,)),
        ],
        compiler_params=pltpu.CompilerParams(
            collective_id=1, has_side_effects=True, vmem_limit_bytes=12 * 2**20),
        name="exchange",
    )(picked)
    return panel.reshape(species, total, width), gram


def per_device(snapshot, species_pick, basis_start):
    axes = ("gx", "gy", "gz")
    devices = lax.axis_size(axes)
    picked = gather(snapshot, species_pick)
    _, species, _, width = picked.shape
    scaling = 1.0 / (species * width * devices)
    panel, gram = exchange(picked, scaling)
    gram_rows, image_rows, image = reduce_and_spread(gram, basis_start)
    basis_rows, core = tail(image, image_rows, panel)
    return gram_rows, basis_rows, core[:, :, None, :]


def solution(mesh):
    return jax.shard_map(
        per_device,
        mesh=mesh,
        in_specs=(P(None, "gz", "gx", "gy"), P(), P()),
        out_specs=(
            P(("gx", "gy", "gz"), None),
            P(("gx", "gy", "gz"), None),
            P(None, None, ("gx", "gz"), "gy"),
        ),
        check_vma=False,
    )
```

```python
import functools

import jax
import jax.numpy as jnp
from jax import lax
from jax.experimental import pallas as pl
from jax.experimental.pallas import tpu as pltpu
from jax.sharding import PartitionSpec as P

HIGHEST = lax.Precision.HIGHEST
F32 = jnp.float32
BF16 = jnp.bfloat16
BLOCK = 128
TILE = 8
PAIR = 2


def split(x):
    high = x.astype(BF16)
    return high, (x - high.astype(F32)).astype(BF16)


def dot(a, b, contract, precision=None):
    return lax.dot_general(
        a, b, (((contract[0],), (contract[1],)), ((), ())),
        precision=precision, preferred_element_type=F32,
    )


def eliminate(read):
    count = BLOCK // TILE
    row = lax.broadcasted_iota(jnp.int32, (TILE, BLOCK), 0)
    lane = lax.broadcasted_iota(jnp.int32, (TILE, BLOCK), 1)
    left = [read(i) for i in range(count)]
    right = [(lane == row + TILE * i).astype(F32) for i in range(count)]

    def wide(x):
        return jnp.broadcast_to(x, (TILE, BLOCK))

    for t in range(count):
        columns = [wide(left[t][:, TILE * t + l:TILE * t + l + 1]) for l in range(TILE)]
        pivots, inverses, upper, lrows, rrows = [], [], [], [], []
        for l in range(TILE):
            pivot = wide(columns[l][l:l + 1, :])
            inverse = 1.0 / pivot
            factor = jnp.where(row > l, columns[l] * inverse, 0.0)
            lrow, rrow = wide(left[t][l:l + 1, :]), wide(right[t][l:l + 1, :])
            ahead = {}
            for m in range(l + 1, TILE):
                ahead[m] = wide(columns[m][l:l + 1, :])
                columns[m] = columns[m] - factor * ahead[m]
            left[t] = left[t] - factor * lrow
            right[t] = right[t] - factor * rrow
            pivots.append(pivot)
            inverses.append(inverse)
            upper.append(ahead)
            lrows.append(lrow)
            rrows.append(rrow)
        for i in range(t + 1, count):
            below = [wide(left[i][:, TILE * t + l:TILE * t + l + 1]) for l in range(TILE)]
            for l in range(TILE):
                factor = below[l] * inverses[l]
                for m in range(l + 1, TILE):
                    below[m] = below[m] - factor * upper[l][m]
                left[i] = left[i] - factor * lrows[l]
                right[i] = right[i] - factor * rrows[l]
        diagonal = pivots[0]
        for l in range(1, TILE):
            diagonal = jnp.where(row == l, pivots[l], diagonal)
        scale = lax.rsqrt(diagonal)
        scale = scale * (1.5 - 0.5 * diagonal * scale * scale)
        right[t] = right[t] * scale
    return right


def tail_kernel(image_ref, rows_ref, panel_ref, basis_ref, core_ref, a_ref, n_ref, w_ref):
    rank = image_ref.shape[1]
    blocks = rank // BLOCK
    image = image_ref[...]
    inner = dot(image, image, (0, 0), HIGHEST)
    for r in range(blocks):
        for c in range(blocks):
            a_ref[r, c] = inner[r * BLOCK:(r + 1) * BLOCK, c * BLOCK:(c + 1) * BLOCK]
            if r != c:
                n_ref[r, c] = jnp.zeros((BLOCK, BLOCK), F32)
            else:
                n_ref[r, c] = (
                    lax.broadcasted_iota(jnp.int32, (BLOCK, BLOCK), 0)
                    == lax.broadcasted_iota(jnp.int32, (BLOCK, BLOCK), 1)
                ).astype(F32)

    @pl.loop(0, blocks)
    def _(b):
        tiles = eliminate(lambda i: a_ref[b, b, TILE * i:TILE * (i + 1), :])
        for i, tile in enumerate(tiles):
            w_ref[TILE * i:TILE * (i + 1), :] = tile
        w = w_ref[...]
        for c in range(blocks):
            n_ref[b, c] = dot(w, n_ref[b, c], (1, 0), HIGHEST)
        for r in range(1, blocks):
            @pl.when(r > b)
            def _():
                a_ref[b, r] = dot(w, a_ref[b, r], (1, 0), HIGHEST)
        for r in range(1, blocks):
            @pl.when(r > b)
            def _():
                factor = a_ref[b, r]
                for c in range(1, blocks):
                    @pl.when(c > b)
                    def _():
                        a_ref[r, c] = a_ref[r, c] - dot(factor, a_ref[b, c], (0, 0), HIGHEST)
                for c in range(blocks - 1):
                    n_ref[r, c] = n_ref[r, c] - dot(factor, n_ref[b, c], (0, 0), HIGHEST)

    inverse = jnp.concatenate(
        [jnp.concatenate([n_ref[r, c] for c in range(blocks)], axis=1) for r in range(blocks)],
        axis=0,
    )
    basis_ref[...] = dot(rows_ref[...], inverse, (1, 1), HIGHEST)
    basis_t = dot(inverse, image, (1, 1), HIGHEST)
    bh, bl = split(basis_t)
    for s in range(panel_ref.shape[0]):
        ph, plo = split(panel_ref[s])
        core_ref[s] = dot(bh, ph, (1, 0)) + dot(bh, plo, (1, 0)) + dot(bl, ph, (1, 0))


def tail(image, rows, panel):
    total, rank = image.shape
    species, _, width = panel.shape
    vmem = pl.BlockSpec(memory_space=pltpu.VMEM)
    blocks = rank // BLOCK
    return pl.pallas_call(
        tail_kernel,
        out_shape=(
            jax.ShapeDtypeStruct(rows.shape, F32),
            jax.ShapeDtypeStruct((species, rank, width), F32),
        ),
        in_specs=[vmem] * 3,
        out_specs=(vmem, vmem),
        scratch_shapes=[
            pltpu.VMEM((blocks, blocks, BLOCK, BLOCK), F32),
            pltpu.VMEM((blocks, blocks, BLOCK, BLOCK), F32),
            pltpu.VMEM((BLOCK, BLOCK), F32),
        ],
        compiler_params=pltpu.CompilerParams(vmem_limit_bytes=24 * 2**20),
        name="tail",
    )(image, rows, panel)


def gather_kernel(pick_ref, in_ref, out_ref):
    for y in range(in_ref.shape[2]):
        out_ref[y, 0] = in_ref[0, :, y, :]


def gather(snapshot, species_pick):
    _, rows, ys, width = snapshot.shape
    species = species_pick.shape[0]
    return pl.pallas_call(
        gather_kernel,
        out_shape=jax.ShapeDtypeStruct((ys, species, rows, width), F32),
        grid_spec=pltpu.PrefetchScalarGridSpec(
            num_scalar_prefetch=1,
            grid=(species,),
            in_specs=[pl.BlockSpec((1, rows, ys, width), lambda s, pick: (pick[s], 0, 0, 0))],
            out_specs=pl.BlockSpec((ys, 1, rows, width), lambda s, pick: (0, s, 0, 0)),
        ),
        name="gather",
    )(species_pick, snapshot)


def reduce_kernel(dims, g_ref, start_ref, rows_ref, own_ref, image_ref,
                  r0, sa, sb, ra1, rb1, ta, tb, ra2, rb2, tz, r3, im, send, recv):
    nx, nh, nl, nz = dims
    gx, gy, gz = lax.axis_index("gx"), lax.axis_index("gy"), lax.axis_index("gz")
    yh, yl = gy // nl, gy % nl
    share, total = rows_ref.shape
    group = nz * share
    half = total // 2
    zhalf = nz // 2
    peers = {
        "x": [((gx + k) % nx, "gx", lambda p: p) for k in range(1, nx)],
        "h": [((yh + k) % nh, "gy", lambda p: p * nl + yl) for k in range(1, nh)],
        "l": [((yl + k) % nl, "gy", lambda p: yh * nl + p) for k in range(1, nl)],
        "z": [((gz + k) % nz, "gz", lambda p: p) for k in range(1, nz)],
    }
    used = [0]

    barrier = pltpu.get_barrier_semaphore()
    count = 0
    for key in "xhlz":
        for p, axis, place in peers[key]:
            pl.semaphore_signal(barrier, inc=1, device_id={axis: place(p)},
                                device_id_type=pl.DeviceIdType.MESH)
            count += 1
    pl.semaphore_wait(barrier, count)

    def exchange(key, source, target):
        copies = []
        for k, (p, axis, place) in enumerate(peers[key]):
            i = used[0]
            used[0] += 1
            copy = pltpu.make_async_remote_copy(
                src_ref=source(p), dst_ref=target(k), send_sem=send.at[i], recv_sem=recv.at[i],
                device_id={axis: place(p)}, device_id_type=pl.DeviceIdType.MESH,
            )
            copy.start()
            copies.append(copy)
        return copies

    def finish(copies):
        for copy in copies:
            copy.wait()

    def plus(first, buffer, count):
        for k in range(count):
            first = first + buffer(k)
        return first

    def part(p, size):
        return pl.ds(pl.multiple_of(p * size, size), size)

    left, right = pl.ds(0, half), pl.ds(half, half)

    def pairs(cut):
        return exchange("l", lambda p: g_ref.at[:, part(p, group), cut], lambda k: r0.at[k, :, :, cut])

    def paired(m, cut):
        return plus(g_ref[m, part(yl, group), cut], lambda k: r0[k, m, :, cut], nl - 1)

    pair_a, pair_b = pairs(left), pairs(right)
    finish(pair_a)
    for m in range(nx * nh):
        sa[m // nh, m % nh] = paired(m, left)
    first_a = exchange("x", lambda p: sa.at[p], lambda k: ra1.at[k])
    finish(pair_b)
    for m in range(nx * nh):
        sb[m % nh, m // nh] = paired(m, right)
    first_b = exchange("h", lambda p: sb.at[p], lambda k: rb1.at[k])
    finish(first_a)
    ta[...] = plus(sa[gx], lambda k: ra1[k], nx - 1)
    second_a = exchange("h", lambda p: ta.at[p], lambda k: ra2.at[k])
    finish(first_b)
    tb[...] = plus(sb[yh], lambda k: rb1[k], nh - 1)
    second_b = exchange("x", lambda p: tb.at[p], lambda k: rb2.at[k])
    def along(cut):
        return exchange("z", lambda p: tz.at[part(p, share), cut], lambda k: r3.at[k, :, cut])

    finish(second_a)
    tz[:, left] = plus(ta[yh], lambda k: ra2[k], nh - 1)
    last_a = along(left)
    finish(second_b)
    tz[:, right] = plus(tb[gx], lambda k: rb2[k], nx - 1)
    last_b = along(right)
    finish(last_a)
    finish(last_b)
    gram = plus(tz[part(gz, share), :], lambda k: r3[k], nz - 1)
    rows_ref[...] = gram
    own = dot(gram, start_ref[...], (1, 0), HIGHEST)
    own_ref[...] = own
    im[gx, yh, yl, gz] = own

    def spread(key, *place):
        return exchange(key, lambda p: im.at[place], lambda k: im.at[place])

    low, high, every = pl.ds(0, zhalf), pl.ds(zhalf, nz - zhalf), slice(None)
    finish(spread("z", gx, yh, yl, gz))
    first_a = spread("x", gx, yh, yl, low)
    first_b = spread("h", gx, yh, yl, high)
    finish(first_a)
    second_a = spread("h", every, yh, yl, low)
    finish(first_b)
    second_b = spread("x", gx, every, yl, high)
    finish(second_a)
    last_a = spread("l", every, every, yl, low)
    finish(second_b)
    last_b = spread("l", every, every, yl, high)
    finish(last_a)
    finish(last_b)
    image_ref[...] = im[...]


def reduce_and_spread(gram, start):
    nx, ny, nz = lax.axis_size("gx"), lax.axis_size("gy"), lax.axis_size("gz")
    nl = 2 if ny % 2 == 0 else 1
    nh = ny // nl
    total, rank = start.shape
    share = total // (nx * ny * nz)
    group, half = nz * share, total // 2
    copies = 4 * ((nl - 1) + (nx - 1) + (nh - 1)) + 3 * (nz - 1)
    vmem = pl.BlockSpec(memory_space=pltpu.VMEM)
    shape = (nx, nh, nl, nz, share, rank)

    def held(*size):
        return pltpu.VMEM(size, F32)

    rows, own, image = pl.pallas_call(
        functools.partial(reduce_kernel, (nx, nh, nl, nz)),
        out_shape=(
            jax.ShapeDtypeStruct((share, total), F32),
            jax.ShapeDtypeStruct((share, rank), F32),
            jax.ShapeDtypeStruct(shape, F32),
        ),
        in_specs=[vmem] * 2,
        out_specs=(vmem,) * 3,
        scratch_shapes=[
            held(max(nl - 1, 1), nx * nh, group, total),
            held(nx, nh, group, half),
            held(nh, nx, group, half),
            held(max(nx - 1, 1), nh, group, half),
            held(max(nh - 1, 1), nx, group, half),
            held(nh, group, half),
            held(nx, group, half),
            held(max(nh - 1, 1), group, half),
            held(max(nx - 1, 1), group, half),
            held(group, total),
            held(max(nz - 1, 1), share, total),
            held(*shape),
            pltpu.SemaphoreType.DMA((copies,)),
            pltpu.SemaphoreType.DMA((copies,)),
        ],
        compiler_params=pltpu.CompilerParams(
            collective_id=0, has_side_effects=True, vmem_limit_bytes=24 * 2**20),
        name="reduce_and_spread",
    )(gram.reshape(nx * nh, nl * group, total), start)
    return rows, own, image.reshape(total, rank)


def exchange_kernel(scaling, picked_ref, panel_ref, gram_ref, high, low, own_sem, send, recv):
    nz, species, rows, width = picked_ref.shape
    chunks = species // PAIR
    gz = lax.axis_index("gz")

    barrier = pltpu.get_barrier_semaphore()
    for k in range(1, nz):
        pl.semaphore_signal(barrier, inc=1, device_id={"gz": (gz + k) % nz},
                            device_id_type=pl.DeviceIdType.MESH)
    own = pltpu.make_async_copy(picked_ref.at[gz], panel_ref.at[:, gz], own_sem)
    own.start()
    pl.semaphore_wait(barrier, nz - 1)

    copies = []
    for j in range(chunks):
        for k in range(1, nz):
            p, i = (gz + k) % nz, len(copies)
            copy = pltpu.make_async_remote_copy(
                src_ref=picked_ref.at[p, pl.ds(PAIR * j, PAIR)],
                dst_ref=panel_ref.at[pl.ds(PAIR * j, PAIR), gz],
                send_sem=send.at[i], recv_sem=recv.at[i],
                device_id={"gz": p}, device_id_type=pl.DeviceIdType.MESH,
            )
            copy.start()
            copies.append(copy)
    own.wait()
    for j in range(chunks):
        for copy in copies[j * (nz - 1):(j + 1) * (nz - 1)]:
            copy.wait_recv()
        for t in range(PAIR):
            upper, lower = split(panel_ref[PAIR * j + t].reshape(nz * rows, width))
            high[:, t * width:(t + 1) * width] = upper
            low[:, t * width:(t + 1) * width] = lower

        @pl.loop(0, nz)
        def _(a):
            here = pl.ds(pl.multiple_of(a * rows, rows), rows)
            ah, al = high[here, :], low[here, :]
            for b in range(nz):
                there = slice(b * rows, (b + 1) * rows)
                bh, bl = high[there, :], low[there, :]
                part = dot(ah, bh, (1, 1)) + (dot(ah, bl, (1, 1)) + dot(al, bh, (1, 1)))
                if j > 0:
                    part = part + gram_ref[here, there]
                if j == chunks - 1:
                    part = part * scaling
                gram_ref[here, there] = part
    for copy in copies:
        copy.wait_send()


def exchange(picked, scaling):
    nz, species, rows, width = picked.shape
    total = nz * rows
    copies = species // PAIR * (nz - 1)
    vmem = pl.BlockSpec(memory_space=pltpu.VMEM)
    panel, gram = pl.pallas_call(
        functools.partial(exchange_kernel, scaling),
        out_shape=(
            jax.ShapeDtypeStruct((species, nz, rows, width), F32),
            jax.ShapeDtypeStruct((total, total), F32),
        ),
        in_specs=[pl.BlockSpec(memory_space=pltpu.HBM)],
        out_specs=(vmem, vmem),
        scratch_shapes=[
            pltpu.VMEM((total, PAIR * width), BF16),
            pltpu.VMEM((total, PAIR * width), BF16),
            pltpu.SemaphoreType.DMA,
            pltpu.SemaphoreType.DMA((copies,)),
            pltpu.SemaphoreType.DMA((copies,)),
        ],
        compiler_params=pltpu.CompilerParams(
            collective_id=1, has_side_effects=True, vmem_limit_bytes=12 * 2**20),
        name="exchange",
    )(picked)
    return panel.reshape(species, total, width), gram


def per_device(snapshot, species_pick, basis_start):
    axes = ("gx", "gy", "gz")
    devices = lax.axis_size(axes)
    picked = gather(snapshot, species_pick)
    _, species, _, width = picked.shape
    scaling = 1.0 / (species * width * devices)
    panel, gram = exchange(picked, scaling)
    gram_rows, image_rows, image = reduce_and_spread(gram, basis_start)
    basis_rows, core = tail(image, image_rows, panel)
    return gram_rows, basis_rows, core[:, :, None, :]


def solution(mesh):
    return jax.shard_map(
        per_device,
        mesh=mesh,
        in_specs=(P(None, "gz", "gx", "gy"), P(), P()),
        out_specs=(
            P(("gx", "gy", "gz"), None),
            P(("gx", "gy", "gz"), None),
            P(None, None, ("gx", "gz"), "gy"),
        ),
        check_vma=False,
    )
```
